32 devices in a mesh: disc: 2 (over x), phi: 16 (over z, y, core).
Axes of the slice: x: 2, y: 2, z: 4, core: 2. Of those that a mesh axis runs over, the one named last changes fastest.
Arguments:
- density: float32 [16, 3072, 1024], P('disc', 'phi'), parts along dimension 0, may hold values from 0.05 to 2
- frag_rate: float32 [16, 3072], P('disc', 'phi'), parts along dimension 0, may hold values from 0.05 to 0.5
- radial_speed: float32 [1024], replicated, may hold values from 0.05 to 0.4
- azimuth_speed: float32 [1024], replicated, may hold values from -0.45 to 0.45
- fraction: float32 [16], P('disc'), parts along dimension 0, may hold values from 0 to 1
- shifts: int32 [16], P('disc'), parts along dimension 0, may hold values from 0 to 3071, as said below
- pivots: int32 [1024], replicated, may hold values from 0 to 1022, as said below
Outputs:
- remapped: float32 [16, 3072, 1024], P('disc', 'phi'), parts along dimension 0
The draws below stay inside these ranges and needn't reach their ends.
There are 2 independent parts, one for each index of `disc`. The reference program is written for one: setup_inputs(seed, part) draws one part's arguments, and reference() takes and returns one part's arrays. A program takes and returns all parts, laid end to end along the dimension named above; an argument that names none is the same for every part. Nothing has to cross between parts.
Inputs may be any that keep to these rules, and one draw needn't show every extreme that they name: `shifts`: each radius moves its dust by this many whole cells toward higher azimuth indices. pivots[0] is 0 and pivots[j] < j for every other bin j.
All inputs are finite; a program needn't handle non-finite values.
Results may differ from the reference program's by a relative error of at most 0.000064.
Values sent between devices are 32-bit elements; how exact they have to be, the bound alone decides.
No kernel may reach another device: no remote copies, remote signals or barrier semaphores. Data moves between devices by JAX's collectives and lax.ppermute only.
A program may use at most 128 MiB of HBM per device.

```python
import math
import jax
import jax.numpy as jnp
from jax import lax

NR = 8
A_DEV = 192
NB = 1024
NA = 3072
N_PHI = 16


def draw_shifts(key, part):
    cycle_size = N_PHI
    bit_count = max((cycle_size - 1).bit_length(), 1)
    key_hops, key_rest = jax.random.split(jax.random.fold_in(key, 7))
    device_hops = jax.random.randint(key_hops, (NR,), 0, cycle_size)
    forced = jnp.left_shift(jnp.int32(1), jnp.arange(NR, dtype=jnp.int32) % bit_count)
    device_hops = jnp.bitwise_or(device_hops, forced) % cycle_size
    cell_rest = jax.random.randint(key_rest, (NR,), 0, A_DEV)
    result = device_hops * A_DEV + cell_rest
    result = jnp.where(jnp.arange(NR) == NR - 1, NA - 1, result)
    return result.astype(jnp.int32)


def draw_pivots(key, part):
    bins = jnp.arange(NB, dtype=jnp.int32)
    result = jax.random.randint(jax.random.fold_in(key, 3), (NB,), 0, jnp.maximum(bins, 1))
    result = jnp.where(bins == NB - 1, NB - 2, result)
    return result.astype(jnp.int32)


def shard_levels(key, shape, shards, least, largest):
    level = 1.0
    for position, blocks in shards:
        steps = jax.random.uniform(jax.random.fold_in(jax.random.fold_in(key, 6), position), (blocks,), jnp.float32, least / len(shards), largest / len(shards))
        level = level * jnp.repeat(jnp.exp(steps), shape[position] // blocks).reshape((-1,) + (1,) * (len(shape) - 1 - position))
    return level


def setup_inputs(seed: int = 0, part: int = 0) -> dict:
    streams_of = jax.random.split(jax.random.key(seed), 8)
    part_keys = jax.random.split(jax.random.fold_in(streams_of[7], part), 8)
    density = jnp.clip(jnp.exp(math.log(2.0) - 3.6888794 * jax.random.uniform(part_keys[0], (NR, NA, NB), jnp.float32) ** shard_levels(part_keys[0], (NR, NA, NB), ((1, 16),), -0.2, 0.2)), 0.05, 2.0)
    frag_rate = jnp.clip(jnp.exp(math.log(0.5) - 2.3025851 * jax.random.uniform(part_keys[1], (NR, NA), jnp.float32) ** shard_levels(part_keys[1], (NR, NA), ((1, 16),), -0.2, 0.2)), 0.05, 0.5)
    radial_speed = jnp.clip(jnp.exp(jax.random.uniform(streams_of[2], (NB,), jnp.float32, math.log(0.05), math.log(0.4))), 0.05, 0.4)
    azimuth_speed = jnp.clip(jax.random.uniform(streams_of[3], (NB,), jnp.float32, -0.45, 0.45), -0.45, 0.45)
    fraction = jnp.clip(jax.random.uniform(part_keys[4], (NR,), jnp.float32, 0.0, 1.0), 0.0, 1.0)
    shifts = draw_shifts(jax.random.fold_in(jax.random.fold_in(streams_of[7], part), 71), part)
    pivots = draw_pivots(jax.random.fold_in(streams_of[7], 71), part)
    return {"density": density, "frag_rate": frag_rate, "radial_speed": radial_speed, "azimuth_speed": azimuth_speed, "fraction": fraction, "shifts": shifts, "pivots": pivots}


def breakup_table(pivots, bins):
    source = lax.broadcasted_iota(jnp.int32, (bins, bins), 0)
    target = lax.broadcasted_iota(jnp.int32, (bins, bins), 1)
    share = 1.0 / (pivots.astype(jnp.float32) + 1.0)
    active = source >= 1
    gain = jnp.where((target <= pivots[:, None]) & active, share[:, None], jnp.float32(0.0))
    loss = jnp.where((target == source) & active, jnp.float32(1.0), jnp.float32(0.0))
    return (gain - loss).astype(jnp.float32)


def roll_cells(field, offset):
    return jnp.roll(field, offset, axis=0)


def reference(density, frag_rate, radial_speed, azimuth_speed, fraction, shifts, pivots):
    inward = jnp.concatenate([density[1:], jnp.zeros_like(density[:1])], axis=0)
    settled = (1.0 - radial_speed) * density + radial_speed * inward
    forward = jnp.maximum(azimuth_speed, 0.0)
    backward = jnp.maximum(-azimuth_speed, 0.0)
    drifted = (1.0 - jnp.abs(azimuth_speed)) * settled + forward * jnp.roll(settled, 1, axis=1) + backward * jnp.roll(settled, -1, axis=1)
    breakup = breakup_table(pivots, NB)
    flat = drifted.reshape(-1, NB)
    gained = jnp.dot(flat, breakup, precision=lax.Precision.HIGHEST, preferred_element_type=jnp.float32).reshape(drifted.shape)
    broken = drifted + frag_rate[:, :, None] * gained
    first = jax.vmap(roll_cells)(broken, shifts)
    second = jax.vmap(roll_cells)(broken, shifts + 1)
    far_weight = fraction[:, None, None]
    return (1.0 - far_weight) * first + far_weight * second
```

```python
import functools

import jax
import jax.numpy as jnp
from jax import lax
from jax.experimental import pallas as pl
from jax.experimental.pallas import tpu as pltpu
from jax.sharding import PartitionSpec as P

PAD = 8


def send(block, axis, by):
    count = lax.axis_size(axis)
    if by % count == 0:
        return block
    return lax.ppermute(block, axis, [(i, (i + by) % count) for i in range(count)])


def step_kernel(
    rest_ref, here_ref, inner_ref, behind_ref, ahead_ref, frag_ref, fraction_ref, rows_ref, pivots_ref,
    out_ref, table, settled, broken, rolled,
):
    radius = pl.program_id(0)
    radii = pl.num_programs(0)
    cells, bins = here_ref.shape[1], here_ref.shape[2]
    full = cells + PAD

    @pl.when(radius == 0)
    def _():
        column = jnp.transpose(jnp.broadcast_to(pivots_ref[...], (8, bins)), (1, 0))[:, :1]
        source = lax.broadcasted_iota(jnp.int32, (bins, bins), 0)
        target = lax.broadcasted_iota(jnp.int32, (bins, bins), 1)
        hit = (target <= column) & (source >= 1)
        table[...] = jnp.where(hit, 1.0, 0.0).astype(jnp.bfloat16)
        settled[...] = jnp.zeros_like(settled)

    speed = rows_ref[0:1, :]
    drift = rows_ref[1:2, :]
    share = rows_ref[2:3, :]
    loss = rows_ref[3:4, :]
    inner_speed = jnp.where(radius == radii - 1, 0.0, speed)
    settled[PAD:full, :] = (1.0 - speed) * here_ref[0] + inner_speed * inner_ref[0]
    behind = behind_ref[...]
    ahead = ahead_ref[...]
    settled[PAD - 2 : PAD, :] = (1.0 - speed) * behind[0, 0] + inner_speed * behind[0, 1]
    settled[full : full + 1, :] = (1.0 - speed) * ahead[0, 0] + inner_speed * ahead[0, 1]

    stay = 1.0 - jnp.abs(drift)
    forward = jnp.maximum(drift, 0.0)
    backward = jnp.maximum(-drift, 0.0)
    drifted = (
        stay * settled[PAD - 1 : full, :]
        + forward * settled[PAD - 2 : full - 1, :]
        + backward * settled[PAD : full + 1, :]
    )
    scaled = drifted * share
    high = scaled.astype(jnp.bfloat16)
    low = (scaled - high.astype(jnp.float32)).astype(jnp.bfloat16)
    gained = jnp.dot(high, table[...], preferred_element_type=jnp.float32)
    gained += jnp.dot(low, table[...], preferred_element_type=jnp.float32)
    lane = lax.broadcasted_iota(jnp.int32, frag_ref.shape, 1)
    frag = jnp.sum(jnp.where(lane == radius, frag_ref[...], 0.0), axis=1, keepdims=True)
    broken[0 : cells + 1, :] = drifted + frag[0 : cells + 1, :] * (gained - loss * drifted)

    far = fraction_ref[radius]
    rest = rest_ref[radius]
    blended = (1.0 - far) * broken[1 : full + 1, :] + far * broken[0:full, :]
    whole = pl.multiple_of(rest // PAD * PAD, PAD)
    rolled[pl.ds(whole, full), :] = pltpu.roll(blended, rest % PAD, 0)
    row = lax.broadcasted_iota(jnp.int32, (cells, bins), 0)
    out_ref[0] = jnp.where(row >= rest, rolled[0:cells, :], rolled[cells : 2 * cells, :])


def step_cells(density, frag_rate, radial_speed, azimuth_speed, fraction, rest, pivots):
    radii, cells, bins = density.shape
    behind = send(density[:, cells - 2 :, :], "phi", 1)
    ahead = send(density[:, :1, :], "phi", -1)
    frag_behind = send(frag_rate[:, cells - 1 :], "phi", 1)

    def with_inner(edge):
        return jnp.stack([edge, jnp.concatenate([edge[1:], edge[:1]], axis=0)], axis=1)

    frag = jnp.concatenate([frag_behind, frag_rate, jnp.zeros((radii, PAD - 1), jnp.float32)], axis=1).T
    bin_index = jnp.arange(bins)
    share = 1.0 / (pivots.astype(jnp.float32) + 1.0)
    rows = jnp.stack([radial_speed, azimuth_speed, share, jnp.where(bin_index >= 1, 1.0, 0.0)])
    return pl.pallas_call(
        step_kernel,
        grid_spec=pltpu.PrefetchScalarGridSpec(
            num_scalar_prefetch=1,
            grid=(radii,),
            in_specs=[
                pl.BlockSpec((1, cells, bins), lambda r, rest: (r, 0, 0)),
                pl.BlockSpec((1, cells, bins), lambda r, rest: (jnp.minimum(r + 1, radii - 1), 0, 0)),
                pl.BlockSpec((1, 2, 2, bins), lambda r, rest: (r, 0, 0, 0)),
                pl.BlockSpec((1, 2, 1, bins), lambda r, rest: (r, 0, 0, 0)),
                pl.BlockSpec((cells + PAD, radii), lambda r, rest: (0, 0)),
                pl.BlockSpec(memory_space=pltpu.SMEM),
                pl.BlockSpec((4, bins), lambda r, rest: (0, 0)),
                pl.BlockSpec((1, bins), lambda r, rest: (0, 0)),
            ],
            out_specs=pl.BlockSpec((1, cells, bins), lambda r, rest: (r, 0, 0)),
            scratch_shapes=[
                pltpu.VMEM((bins, bins), jnp.bfloat16),
                pltpu.VMEM((cells + 2 * PAD, bins), jnp.float32),
                pltpu.VMEM((cells + 2 * PAD, bins), jnp.float32),
                pltpu.VMEM((2 * cells, bins), jnp.float32),
            ],
        ),
        out_shape=jax.ShapeDtypeStruct((radii, cells, bins), jnp.float32),
        compiler_params=pltpu.CompilerParams(vmem_limit_bytes=32 * 1024 * 1024),
        cost_estimate=pl.CostEstimate(
            flops=4 * radii * cells * bins * bins, bytes_accessed=12 * radii * cells * bins, transcendentals=0
        ),
    )(rest, density, density, with_inner(behind), with_inner(ahead), frag, fraction, rows, pivots.reshape(1, bins))


def move_block(hops, bucket, step, block, rest):
    cells, bins = block.shape
    start, stop = step * bucket, min(step * bucket + step, cells)
    near = send(block[start:], "phi", hops)
    far = send(block[:stop], "phi", hops + 1)
    row = lax.broadcasted_iota(jnp.int32, (stop - start, bins), 0) + start
    mixed = jnp.where(row < rest, far[start:], near[: stop - start])
    return jnp.concatenate([far[:start], mixed, near[stop - start :]], axis=0)


def body(density, frag_rate, radial_speed, azimuth_speed, fraction, shifts, pivots):
    radii, cells, bins = density.shape
    count = lax.axis_size("phi")
    hops, rest = shifts // cells, shifts % cells
    step = 16 if count <= 16 else 48
    buckets = cells // step
    blocks = step_cells(density, frag_rate, radial_speed, azimuth_speed, fraction, rest, pivots)
    branches = [functools.partial(move_block, h, k, step) for h in range(count) for k in range(buckets)]
    choice = hops * buckets + rest // step

    def move(radius, out):
        block = lax.dynamic_index_in_dim(blocks, radius, 0, keepdims=False)
        moved = lax.switch(choice[radius], branches, block, rest[radius])
        return lax.dynamic_update_index_in_dim(out, moved, radius, 0)

    return lax.fori_loop(0, radii, move, jnp.zeros_like(density))


def solution(mesh):
    placed = (P("disc", "phi", None), P("disc", "phi"), P(), P(), P("disc"), P("disc"), P())
    return jax.shard_map(
        body, mesh=mesh, in_specs=placed, out_specs=P("disc", "phi", None), check_vma=False
    )
```

```python
import functools

import jax
import jax.numpy as jnp
from jax import lax
from jax.experimental import pallas as pl
from jax.experimental.pallas import tpu as pltpu
from jax.sharding import PartitionSpec as P

PAD = 8
UNIT = 64


def send(block, axis, by):
    count = lax.axis_size(axis)
    return lax.ppermute(block, axis, [(i, (i + by) % count) for i in range(count)])


class Plan:
    def __init__(self, radii):
        self.hop = 0
        self.offset = radii
        self.ahead = 2 * radii
        self.behind = 3 * radii
        self.ahead_units = 4 * radii
        self.behind_units = 4 * radii + 1
        self.length = 4 * radii + 2


def write_plan(plan, shifts_ref, plan_ref, radii, cells, count):
    half = cells // 2
    ahead_rows = behind_rows = jnp.int32(0)
    for r in range(radii):
        shift = shifts_ref[r]
        hop = (shift + half) // cells
        offset = shift - hop * cells
        plan_ref[plan.hop + r] = jnp.where(hop >= count, hop - count, hop)
        plan_ref[plan.offset + r] = offset
        plan_ref[plan.ahead + r] = ahead_rows
        plan_ref[plan.behind + r] = behind_rows
        ahead_rows = ahead_rows + jnp.where(offset > 0, (offset + 7) // 8 * 8, 0)
        behind_rows = behind_rows + jnp.where(offset < 0, (7 - offset) // 8 * 8, 0)
    plan_ref[plan.ahead_units] = (ahead_rows + (UNIT - 1)) // UNIT
    plan_ref[plan.behind_units] = (behind_rows + (UNIT - 1)) // UNIT


def step_kernel(plan, count, radii, *refs):
    (shifts_ref, here_ref, inner_ref, behind_ref, ahead_ref, frag_ref, fraction_ref, rows_ref, pivots_ref) = refs[:9]
    out_refs = refs[9 : 9 + radii]
    plan_ref, table, settled, broken, rolled, turned, sems = refs[9 + radii :]
    radius = pl.program_id(0)
    cells, bins = here_ref.shape[1], here_ref.shape[2]
    full = cells + PAD

    @pl.when(radius == 0)
    def _():
        column = jnp.transpose(jnp.broadcast_to(pivots_ref[...], (8, bins)), (1, 0))[:, :1]
        source = lax.broadcasted_iota(jnp.int32, (bins, bins), 0)
        target = lax.broadcasted_iota(jnp.int32, (bins, bins), 1)
        hit = (target <= column) & (source >= 1)
        table[...] = jnp.where(hit, 1.0, 0.0).astype(jnp.bfloat16)
        settled[...] = jnp.zeros_like(settled)
        write_plan(plan, shifts_ref, plan_ref, radii, cells, count)

    speed = rows_ref[0:1, :]
    drift = rows_ref[1:2, :]
    share = rows_ref[2:3, :]
    loss = rows_ref[3:4, :]
    inner_speed = jnp.where(radius == radii - 1, 0.0, speed)
    settled[PAD:full, :] = (1.0 - speed) * here_ref[0] + inner_speed * inner_ref[0]
    behind = behind_ref[...]
    ahead = ahead_ref[...]
    settled[PAD - 2 : PAD, :] = (1.0 - speed) * behind[0, 0] + inner_speed * behind[0, 1]
    settled[full : full + 1, :] = (1.0 - speed) * ahead[0, 0] + inner_speed * ahead[0, 1]

    stay = 1.0 - jnp.abs(drift)
    forward = jnp.maximum(drift, 0.0)
    backward = jnp.maximum(-drift, 0.0)
    drifted = (
        stay * settled[PAD - 1 : full, :]
        + forward * settled[PAD - 2 : full - 1, :]
        + backward * settled[PAD : full + 1, :]
    )
    scaled = drifted * share
    high = scaled.astype(jnp.bfloat16)
    low = (scaled - high.astype(jnp.float32)).astype(jnp.bfloat16)
    gained = jnp.dot(high, table[...], preferred_element_type=jnp.float32)
    gained += jnp.dot(low, table[...], preferred_element_type=jnp.float32)
    lane = lax.broadcasted_iota(jnp.int32, frag_ref.shape, 1)
    frag = jnp.sum(jnp.where(lane == radius, frag_ref[...], 0.0), axis=1, keepdims=True)
    broken[0 : cells + 1, :] = drifted + frag[0 : cells + 1, :] * (gained - loss * drifted)

    far = fraction_ref[radius]
    offset = plan_ref[plan.offset + radius]
    rest = jnp.where(offset < 0, offset + cells, offset)
    blended = (1.0 - far) * broken[1 : full + 1, :] + far * broken[0:full, :]
    whole = pl.multiple_of(rest // PAD * PAD, PAD)
    rolled[pl.ds(whole, full), :] = pltpu.roll(blended, rest % PAD, 0)
    row = lax.broadcasted_iota(jnp.int32, (cells, bins), 0)

    for r in range(radii):

        @pl.when(radius == r)
        def _(r=r):
            slot = r % 2
            if r >= 2:
                pltpu.make_async_copy(turned.at[slot], out_refs[r - 2], sems.at[slot]).wait()
            turned[slot] = jnp.where(row >= rest, rolled[0:cells, :], rolled[cells : 2 * cells, :])
            pltpu.make_async_copy(turned.at[slot], out_refs[r], sems.at[slot]).start()
            if r == radii - 1:
                for last in range(max(radii - 2, 0), radii):
                    pltpu.make_async_copy(turned.at[last % 2], out_refs[last], sems.at[last % 2]).wait()


def step_cells(density, frag_rate, radial_speed, azimuth_speed, fraction, shifts, pivots, plan, count):
    radii, cells, bins = density.shape
    behind = send(density[:, cells - 2 :, :], "phi", 1)
    ahead = send(density[:, :1, :], "phi", -1)
    frag_behind = send(frag_rate[:, cells - 1 :], "phi", 1)

    def with_inner(edge):
        return jnp.stack([edge, jnp.concatenate([edge[1:], edge[:1]], axis=0)], axis=1)

    frag = jnp.concatenate([frag_behind, frag_rate, jnp.zeros((radii, PAD - 1), jnp.float32)], axis=1).T
    bin_index = jnp.arange(bins)
    share = 1.0 / (pivots.astype(jnp.float32) + 1.0)
    rows = jnp.stack([radial_speed, azimuth_speed, share, jnp.where(bin_index >= 1, 1.0, 0.0)])
    anywhere = pl.BlockSpec(memory_space=pl.ANY)
    return pl.pallas_call(
        functools.partial(step_kernel, plan, count, radii),
        grid_spec=pltpu.PrefetchScalarGridSpec(
            num_scalar_prefetch=1,
            grid=(radii,),
            in_specs=[
                pl.BlockSpec((1, cells, bins), lambda r, s: (r, 0, 0)),
                pl.BlockSpec((1, cells, bins), lambda r, s: (jnp.minimum(r + 1, radii - 1), 0, 0)),
                pl.BlockSpec((1, 2, 2, bins), lambda r, s: (r, 0, 0, 0)),
                pl.BlockSpec((1, 2, 1, bins), lambda r, s: (r, 0, 0, 0)),
                pl.BlockSpec((cells + PAD, radii), lambda r, s: (0, 0)),
                pl.BlockSpec(memory_space=pltpu.SMEM),
                pl.BlockSpec((4, bins), lambda r, s: (0, 0)),
                pl.BlockSpec((1, bins), lambda r, s: (0, 0)),
            ],
            out_specs=[anywhere] * radii + [pl.BlockSpec(memory_space=pltpu.SMEM)],
            scratch_shapes=[
                pltpu.VMEM((bins, bins), jnp.bfloat16),
                pltpu.VMEM((cells + 2 * PAD, bins), jnp.float32),
                pltpu.VMEM((cells + 2 * PAD, bins), jnp.float32),
                pltpu.VMEM((2 * cells, bins), jnp.float32),
                pltpu.VMEM((2, cells, bins), jnp.float32),
                pltpu.SemaphoreType.DMA((2,)),
            ],
        ),
        out_shape=[jax.ShapeDtypeStruct((cells, bins), jnp.float32)] * radii
        + [jax.ShapeDtypeStruct((plan.length,), jnp.int32)],
        compiler_params=pltpu.CompilerParams(vmem_limit_bytes=40 * 1024 * 1024),
        cost_estimate=pl.CostEstimate(
            flops=4 * radii * cells * bins * bins, bytes_accessed=12 * radii * cells * bins, transcendentals=0
        ),
    )(shifts, density, density, with_inner(behind), with_inner(ahead), frag, fraction, rows, pivots.reshape(1, bins))


def piece_sizes(half):
    size = PAD
    while size * 2 <= half:
        size *= 2
    while size >= PAD:
        yield size
        size //= 2


def each_piece(rows, source, target, half, act):
    done = jnp.int32(0)
    for size in piece_sizes(half):
        take = (rows // size) % 2 == 1
        start = done

        @pl.when(take)
        def _(size=size, start=start):
            act(pl.multiple_of(source + start, PAD), pl.multiple_of(target + start, PAD), size)

        done = done + jnp.where(take, size, 0)


def pack_kernel(plan, radii, plan_ref, *refs):
    field_refs = refs[:radii]
    to_next_ref, to_last_ref, edge, read_sem, write_sem = refs[radii:]
    half = edge.shape[1]
    for r in range(radii):
        offset = plan_ref[plan.offset + r]

        @pl.when(offset > 0)
        def _(r=r):
            pltpu.make_async_copy(field_refs[r].at[pl.ds(0, half)], edge.at[r], read_sem.at[r]).start()

        @pl.when(offset <= 0)
        def _(r=r):
            pltpu.make_async_copy(field_refs[r].at[pl.ds(half, half)], edge.at[r], read_sem.at[r]).start()

    def pieces(r, act):
        offset = plan_ref[plan.offset + r]
        to_next = jnp.where(offset > 0, (offset + 7) // 8 * 8, 0)
        to_last = jnp.where(offset < 0, (7 - offset) // 8 * 8, 0)

        def copy(target_ref):
            def run(source, target, size):
                act(
                    pltpu.make_async_copy(
                        edge.at[r, pl.ds(source, size)], target_ref.at[pl.ds(target, size)], write_sem.at[r]
                    )
                )

            return run

        each_piece(to_next, 0, plan_ref[plan.ahead + r], half, copy(to_next_ref))
        each_piece(to_last, half - to_last, plan_ref[plan.behind + r], half, copy(to_last_ref))

    for r in range(radii):
        pltpu.make_async_copy(field_refs[r].at[pl.ds(0, half)], edge.at[r], read_sem.at[r]).wait()
        pieces(r, lambda copy: copy.start())
    for r in range(radii):
        pieces(r, lambda copy: copy.wait())


def pack(plan, steer, fields):
    radii = len(fields)
    cells, bins = fields[0].shape
    half = cells // 2
    anywhere = pl.BlockSpec(memory_space=pl.ANY)
    packed = jax.ShapeDtypeStruct((radii * half, bins), jnp.float32)
    return pl.pallas_call(
        functools.partial(pack_kernel, plan, radii),
        grid_spec=pltpu.PrefetchScalarGridSpec(
            num_scalar_prefetch=1,
            grid=(),
            in_specs=[anywhere] * radii,
            out_specs=[anywhere] * 2,
            scratch_shapes=[
                pltpu.VMEM((radii, half, bins), jnp.float32),
                pltpu.SemaphoreType.DMA((radii,)),
                pltpu.SemaphoreType.DMA((radii,)),
            ],
        ),
        out_shape=[packed, packed],
    )(steer, *fields)


def exchange(packed, by, lead, units):
    limit = packed.shape[0]

    def send_units(n, packed):
        rows = min(n * UNIT, limit)
        if rows == 0:
            return jnp.zeros((lead + limit, packed.shape[1]), jnp.float32)
        return jnp.pad(send(packed[:rows], "phi", by), ((lead, limit - rows), (0, 0)))

    branches = [functools.partial(send_units, n) for n in range(-(-limit // UNIT) + 1)]
    return lax.switch(units, branches, packed)


def patch_kernel(plan, radii, plan_ref, *refs):
    field_refs = refs[:radii]
    from_last_ref, from_next_ref, out_ref, held, edge, read_sem, edge_sem, write_sem = refs[radii:]
    half, bins = edge.shape[1], edge.shape[2]
    for r in range(radii):
        offset = plan_ref[plan.offset + r]
        pltpu.make_async_copy(field_refs[r], held.at[r], read_sem.at[r]).start()

        @pl.when(offset > 0)
        def _(r=r):
            start = pl.multiple_of(plan_ref[plan.ahead + r], PAD)
            pltpu.make_async_copy(from_last_ref.at[pl.ds(start, half)], edge.at[r], edge_sem.at[r]).start()

        @pl.when(offset <= 0)
        def _(r=r, offset=offset):
            rows = jnp.where(offset < 0, (7 - offset) // 8 * 8, 0)
            start = pl.multiple_of(plan_ref[plan.behind + r] + rows, PAD)
            pltpu.make_async_copy(from_next_ref.at[pl.ds(start, half)], edge.at[r], edge_sem.at[r]).start()

    row = lax.broadcasted_iota(jnp.int32, (half, bins), 0)
    for r in range(radii):
        offset = plan_ref[plan.offset + r]
        pltpu.make_async_copy(field_refs[r], held.at[r], read_sem.at[r]).wait()
        pltpu.make_async_copy(from_last_ref.at[pl.ds(0, half)], edge.at[r], edge_sem.at[r]).wait()

        @pl.when(offset > 0)
        def _(r=r, offset=offset):
            held[r, :half, :] = jnp.where(row < offset, edge[r], held[r, :half, :])

        @pl.when(offset < 0)
        def _(r=r, offset=offset):
            held[r, half:, :] = jnp.where(row >= half + offset, edge[r], held[r, half:, :])

        pltpu.make_async_copy(held.at[r], out_ref.at[r], write_sem.at[r]).start()
    for r in range(radii):
        pltpu.make_async_copy(held.at[r], out_ref.at[r], write_sem.at[r]).wait()


def patch(plan, steer, fields, from_last, from_next):
    radii = len(fields)
    cells, bins = fields[0].shape
    half = cells // 2
    anywhere = pl.BlockSpec(memory_space=pl.ANY)
    return pl.pallas_call(
        functools.partial(patch_kernel, plan, radii),
        grid_spec=pltpu.PrefetchScalarGridSpec(
            num_scalar_prefetch=1,
            grid=(),
            in_specs=[anywhere] * (radii + 2),
            out_specs=anywhere,
            scratch_shapes=[
                pltpu.VMEM((radii, cells, bins), jnp.float32),
                pltpu.VMEM((radii, half, bins), jnp.float32),
                pltpu.SemaphoreType.DMA((radii,)),
                pltpu.SemaphoreType.DMA((radii,)),
                pltpu.SemaphoreType.DMA((radii,)),
            ],
        ),
        out_shape=jax.ShapeDtypeStruct((radii, cells, bins), jnp.float32),
    )(steer, *fields, from_last, from_next)


def body(density, frag_rate, radial_speed, azimuth_speed, fraction, shifts, pivots):
    radii, cells, bins = density.shape
    count = lax.axis_size("phi")
    plan = Plan(radii)
    *fields, steer = step_cells(
        density, frag_rate, radial_speed, azimuth_speed, fraction, shifts, pivots, plan, count
    )
    branches = [functools.partial(send, axis="phi", by=by) for by in range(count)]
    fields = [lax.switch(steer[plan.hop + r], branches, field) for r, field in enumerate(fields)]
    to_next, to_last = pack(plan, steer, fields)
    from_last = exchange(to_next, 1, 0, steer[plan.ahead_units])
    from_next = exchange(to_last, -1, cells // 2, steer[plan.behind_units])
    return patch(plan, steer, fields, from_last, from_next)


def solution(mesh):
    placed = (P("disc", "phi", None), P("disc", "phi"), P(), P(), P("disc"), P("disc"), P())
    return jax.shard_map(
        body, mesh=mesh, in_specs=placed, out_specs=P("disc", "phi", None), check_vma=False
    )
```

```python
import functools

import jax
import jax.numpy as jnp
from jax import lax
from jax.experimental import pallas as pl
from jax.experimental.pallas import tpu as pltpu
from jax.sharding import PartitionSpec as P

PAD = 8
UNIT = 64


def send(block, axis, by):
    count = lax.axis_size(axis)
    return lax.ppermute(block, axis, [(i, (i + by) % count) for i in range(count)])


class Plan:
    def __init__(self, radii):
        self.offset = 0
        self.ahead = radii
        self.behind = 2 * radii
        self.ahead_units = 3 * radii
        self.behind_units = 3 * radii + 1
        self.length = 3 * radii + 2


def write_plan(plan, shifts_ref, plan_ref, radii, cells):
    half = cells // 2
    ahead_rows = behind_rows = jnp.int32(0)
    for r in range(radii):
        shift = shifts_ref[r]
        hop = (shift + half) // cells
        offset = shift - hop * cells
        plan_ref[plan.offset + r] = offset
        plan_ref[plan.ahead + r] = ahead_rows
        plan_ref[plan.behind + r] = behind_rows
        ahead_rows = ahead_rows + jnp.where(offset > 0, (offset + 7) // 8 * 8, 0)
        behind_rows = behind_rows + jnp.where(offset < 0, (7 - offset) // 8 * 8, 0)
    plan_ref[plan.ahead_units] = (ahead_rows + (UNIT - 1)) // UNIT
    plan_ref[plan.behind_units] = (behind_rows + (UNIT - 1)) // UNIT


def pick(index, branches, operand):
    traced = jax.make_jaxpr(lambda i, x: lax.switch(i, branches, x))(index, operand)
    (choice,) = [eqn for eqn in traced.eqns if eqn.primitive is lax.cond_p]
    (result,) = choice.primitive.bind(index, operand, **choice.params)
    return result


def step_kernel(plan, radii, *refs):
    (shifts_ref, here_ref, inner_ref, behind_ref, ahead_ref, frag_ref, frag_behind_ref) = refs[:7]
    (fraction_ref, speed_ref, drift_ref, pivots_ref) = refs[7:11]
    out_refs = refs[11 : 11 + radii]
    plan_ref, table, rows, column, settled, drifted, split, gained, turned, sems = refs[11 + radii :]
    radius = pl.program_id(0)
    cells, bins = here_ref.shape[1], here_ref.shape[2]
    tile = 2 * PAD
    full = settled.shape[0]

    @pl.when(radius == 0)
    def _():
        pivots = jnp.transpose(jnp.broadcast_to(pivots_ref[...], (8, bins)), (1, 0))[:, :1]
        source = lax.broadcasted_iota(jnp.int32, (bins, bins), 0)
        target = lax.broadcasted_iota(jnp.int32, (bins, bins), 1)
        hit = (target <= pivots) & (source >= 1)
        write_plan(plan, shifts_ref, plan_ref, radii, cells)
        table[...] = jnp.where(hit, 1.0, 0.0).astype(jnp.bfloat16)
        settled[0:PAD, :] = jnp.zeros((PAD, bins), jnp.float32)
        settled[PAD + cells : full, :] = jnp.zeros((full - PAD - cells, bins), jnp.float32)
        drift = drift_ref[...]
        lane = lax.broadcasted_iota(jnp.int32, (1, bins), 1)
        rows[0:1, :] = 1.0 - jnp.abs(drift)
        rows[1:2, :] = jnp.maximum(drift, 0.0)
        rows[2:3, :] = jnp.maximum(-drift, 0.0)
        rows[3:4, :] = 1.0 / (pivots_ref[...].astype(jnp.float32) + 1.0)
        rows[4:5, :] = jnp.where(lane >= 1, 1.0, 0.0)
        column[0:PAD, :] = jnp.transpose(frag_behind_ref[...], (1, 0))[cells - PAD :, :]
        column[PAD : PAD + cells, :] = jnp.transpose(frag_ref[...], (1, 0))

    inner = jnp.minimum(radius + 1, radii - 1)
    speed = speed_ref[...]
    keep = 1.0 - speed
    inner_speed = jnp.where(radius == radii - 1, 0.0, speed)
    settled[PAD - 2 : PAD, :] = keep * behind_ref[radius] + inner_speed * behind_ref[inner]
    settled[PAD + cells : PAD + cells + 1, :] = keep * ahead_ref[radius] + inner_speed * ahead_ref[inner]

    def settle(t, _):
        start = pl.multiple_of(t * tile, tile)
        now = keep * here_ref[0, pl.ds(start, tile), :] + inner_speed * inner_ref[0, pl.ds(start, tile), :]
        settled[pl.ds(pl.multiple_of(start + PAD, PAD), tile), :] = now
        return 0

    lax.fori_loop(0, cells // tile, settle, 0, unroll=True)

    stay, forward, backward, share = rows[0:1, :], rows[1:2, :], rows[2:3, :], rows[3:4, :]
    low_start = split.shape[0] // 2

    def spread(t, _):
        start = pl.multiple_of(t * tile, tile)
        now = settled[pl.ds(start, tile), :]
        before = settled[pl.ds(pl.multiple_of(jnp.maximum(start - PAD, 0), PAD), PAD), :]
        after = settled[pl.ds(pl.multiple_of(jnp.minimum(start + tile, full - PAD), PAD), PAD), :]
        row = lax.broadcasted_iota(jnp.int32, (tile, bins), 0)
        down = jnp.where(row == 0, before[PAD - 1 :, :], pltpu.roll(now, 1, 0))
        up = jnp.where(row == tile - 1, after[:1, :], pltpu.roll(now, tile - 1, 0))
        moved = stay * now + forward * down + backward * up
        drifted[pl.ds(start, tile), :] = moved
        scaled = moved * share
        high = scaled.astype(jnp.bfloat16)
        split[pl.ds(start, tile), :] = high
        split[pl.ds(pl.multiple_of(low_start + start, tile), tile), :] = (
            scaled - high.astype(jnp.float32)
        ).astype(jnp.bfloat16)
        return 0

    lax.fori_loop(0, full // tile, spread, 0, unroll=True)

    width = min(256, bins)

    for start in range(0, bins, width):
        part = slice(start, start + width)
        gained[:, part] = jnp.dot(
            split[:, start:], table[start:, part], preferred_element_type=jnp.float32
        )

    far = fraction_ref[radius]
    shift = shifts_ref[radius]
    rest = lax.rem(shift, cells)
    whole = rest // PAD
    odd = rest - whole * PAD
    loss = rows[4:5, :]
    lane = lax.broadcasted_iota(jnp.int32, (PAD, radii), 1)
    row = lax.broadcasted_iota(jnp.int32, (PAD, bins), 0)

    def broken(u):
        here = pl.ds(pl.multiple_of(u * PAD, PAD), PAD)
        low = pl.ds(pl.multiple_of(low_start + u * PAD, PAD), PAD)
        now = drifted[here, :]
        frag = jnp.sum(jnp.where(lane == radius, column[here, :], 0.0), axis=1, keepdims=True)
        return now + frag * (gained[here, :] + gained[low, :] - loss * now)

    def blend(u, before):
        now = broken(u)
        mixed = jnp.where(row == 0, before, pltpu.roll(now, 1, 0))
        return pltpu.roll((1.0 - far) * now + far * mixed, odd, 0), now[PAD - 1 :, :]

    tiles = cells // PAD

    def finish(slot):
        first = broken(jnp.int32(0))[PAD - 1 :, :]
        head, before = blend(jnp.int32(1), first)

        def put(u, turn):
            place = whole + u
            place = jnp.where(place >= tiles, place - tiles, place)
            turned[slot, pl.ds(pl.multiple_of(place * PAD, PAD), PAD), :] = turn

        def one(u, carry):
            last, before = carry
            turn, before = blend(u + 1, before)
            put(u, jnp.where(row < odd, last, turn))
            return turn, before

        last, _ = lax.fori_loop(1, tiles, one, (head, before), unroll=True)
        put(jnp.int32(0), jnp.where(row < odd, last, head))

    slot = lax.rem(radius, 2)
    for r in range(2, radii):

        @pl.when(radius == r)
        def _(r=r):
            pltpu.make_async_copy(turned.at[r % 2], out_refs[r - 2], sems.at[r % 2]).wait()

    finish(slot)
    for r in range(radii):

        @pl.when(radius == r)
        def _(r=r):
            pltpu.make_async_copy(turned.at[r % 2], out_refs[r], sems.at[r % 2]).start()
            if r == radii - 1:
                for last in range(max(radii - 2, 0), radii):
                    pltpu.make_async_copy(turned.at[last % 2], out_refs[last], sems.at[last % 2]).wait()


def step_cells(density, frag_rate, radial_speed, azimuth_speed, fraction, shifts, pivots, plan):
    radii, cells, bins = density.shape
    frag_behind = send(frag_rate, "phi", 1)
    behind = send(density[:, cells - 2 :, :], "phi", 1)
    ahead = send(density[:, :1, :], "phi", -1)
    anywhere = pl.BlockSpec(memory_space=pl.ANY)
    full = cells + 2 * PAD

    def fixed(*shape):
        return pl.BlockSpec(shape, lambda r, s: (0,) * len(shape))

    return pl.pallas_call(
        functools.partial(step_kernel, plan, radii),
        grid_spec=pltpu.PrefetchScalarGridSpec(
            num_scalar_prefetch=1,
            grid=(radii,),
            in_specs=[
                pl.BlockSpec((1, cells, bins), lambda r, s: (r, 0, 0)),
                pl.BlockSpec((1, cells, bins), lambda r, s: (jnp.minimum(r + 1, radii - 1), 0, 0)),
                fixed(radii, 2, bins),
                fixed(radii, 1, bins),
                fixed(radii, cells),
                fixed(radii, cells),
                pl.BlockSpec(memory_space=pltpu.SMEM),
                fixed(1, bins),
                fixed(1, bins),
                fixed(1, bins),
            ],
            out_specs=[anywhere] * radii + [pl.BlockSpec(memory_space=pltpu.SMEM)],
            scratch_shapes=[
                pltpu.VMEM((bins, bins), jnp.bfloat16),
                pltpu.VMEM((PAD, bins), jnp.float32),
                pltpu.VMEM((full, radii), jnp.float32),
                pltpu.VMEM((full, bins), jnp.float32),
                pltpu.VMEM((full, bins), jnp.float32),
                pltpu.VMEM((2 * full, bins), jnp.bfloat16),
                pltpu.VMEM((2 * full, bins), jnp.float32),
                pltpu.VMEM((2, cells, bins), jnp.float32),
                pltpu.SemaphoreType.DMA((2,)),
            ],
        ),
        out_shape=[jax.ShapeDtypeStruct((cells, bins), jnp.float32)] * radii
        + [jax.ShapeDtypeStruct((plan.length,), jnp.int32)],
        compiler_params=pltpu.CompilerParams(vmem_limit_bytes=60 * 1024 * 1024),
        cost_estimate=pl.CostEstimate(
            flops=4 * radii * cells * bins * bins, bytes_accessed=12 * radii * cells * bins, transcendentals=0
        ),
    )(
        shifts, density, density, behind, ahead, frag_rate, frag_behind, fraction,
        radial_speed.reshape(1, bins), azimuth_speed.reshape(1, bins), pivots.reshape(1, bins),
    )


def piece_sizes(half):
    size = PAD
    while size * 2 <= half:
        size *= 2
    while size >= PAD:
        yield size
        size //= 2


def each_piece(rows, source, target, half, act):
    done = jnp.int32(0)
    for size in piece_sizes(half):
        take = (rows // size) % 2 == 1
        start = done

        @pl.when(take)
        def _(size=size, start=start):
            act(pl.multiple_of(source + start, PAD), pl.multiple_of(target + start, PAD), size)

        done = done + jnp.where(take, size, 0)


def pack_kernel(plan, radii, plan_ref, *refs):
    field_refs = refs[:radii]
    to_next_ref, to_last_ref, edge, read_sem, write_sem = refs[radii:]
    half = edge.shape[1]
    for r in range(radii):
        offset = plan_ref[plan.offset + r]

        @pl.when(offset > 0)
        def _(r=r):
            pltpu.make_async_copy(field_refs[r].at[pl.ds(0, half)], edge.at[r], read_sem.at[r]).start()

        @pl.when(offset <= 0)
        def _(r=r):
            pltpu.make_async_copy(field_refs[r].at[pl.ds(half, half)], edge.at[r], read_sem.at[r]).start()

    def pieces(r, act):
        offset = plan_ref[plan.offset + r]
        to_next = jnp.where(offset > 0, (offset + 7) // 8 * 8, 0)
        to_last = jnp.where(offset < 0, (7 - offset) // 8 * 8, 0)

        def copy(target_ref):
            def run(source, target, size):
                act(
                    pltpu.make_async_copy(
                        edge.at[r, pl.ds(source, size)], target_ref.at[pl.ds(target, size)], write_sem.at[r]
                    )
                )

            return run

        each_piece(to_next, 0, plan_ref[plan.ahead + r], half, copy(to_next_ref))
        each_piece(to_last, half - to_last, plan_ref[plan.behind + r], half, copy(to_last_ref))

    for r in range(radii):
        pltpu.make_async_copy(field_refs[r].at[pl.ds(0, half)], edge.at[r], read_sem.at[r]).wait()
        pieces(r, lambda copy: copy.start())
    for r in range(radii):
        pieces(r, lambda copy: copy.wait())


def pack(plan, steer, fields):
    radii = len(fields)
    cells, bins = fields[0].shape
    half = cells // 2
    anywhere = pl.BlockSpec(memory_space=pl.ANY)
    packed = jax.ShapeDtypeStruct((radii * half, bins), jnp.float32)
    return pl.pallas_call(
        functools.partial(pack_kernel, plan, radii),
        grid_spec=pltpu.PrefetchScalarGridSpec(
            num_scalar_prefetch=1,
            grid=(),
            in_specs=[anywhere] * radii,
            out_specs=[anywhere] * 2,
            scratch_shapes=[
                pltpu.VMEM((radii, half, bins), jnp.float32),
                pltpu.SemaphoreType.DMA((radii,)),
                pltpu.SemaphoreType.DMA((radii,)),
            ],
        ),
        out_shape=[packed, packed],
    )(steer, *fields)


def exchange(packed, by, lead, units):
    limit = packed.shape[0]

    def send_units(n, packed):
        rows = min(n * UNIT, limit)
        if rows == 0:
            return jnp.zeros((lead + limit, packed.shape[1]), jnp.float32)
        return jnp.pad(send(packed[:rows], "phi", by), ((lead, limit - rows), (0, 0)))

    branches = [functools.partial(send_units, n) for n in range(-(-limit // UNIT) + 1)]
    return pick(units, branches, packed)


def patch_kernel(plan, radii, plan_ref, *refs):
    field_refs = refs[:radii]
    from_last_ref, from_next_ref, out_ref, held, edge, read_sem, edge_sem, write_sem = refs[radii:]
    half, bins = edge.shape[1], edge.shape[2]
    for r in range(radii):
        offset = plan_ref[plan.offset + r]
        pltpu.make_async_copy(field_refs[r], held.at[r], read_sem.at[r]).start()

        @pl.when(offset > 0)
        def _(r=r):
            start = pl.multiple_of(plan_ref[plan.ahead + r], PAD)
            pltpu.make_async_copy(from_last_ref.at[pl.ds(start, half)], edge.at[r], edge_sem.at[r]).start()

        @pl.when(offset <= 0)
        def _(r=r, offset=offset):
            rows = jnp.where(offset < 0, (7 - offset) // 8 * 8, 0)
            start = pl.multiple_of(plan_ref[plan.behind + r] + rows, PAD)
            pltpu.make_async_copy(from_next_ref.at[pl.ds(start, half)], edge.at[r], edge_sem.at[r]).start()

    row = lax.broadcasted_iota(jnp.int32, (half, bins), 0)
    for r in range(radii):
        offset = plan_ref[plan.offset + r]
        pltpu.make_async_copy(field_refs[r], held.at[r], read_sem.at[r]).wait()
        pltpu.make_async_copy(from_last_ref.at[pl.ds(0, half)], edge.at[r], edge_sem.at[r]).wait()

        @pl.when(offset > 0)
        def _(r=r, offset=offset):
            held[r, :half, :] = jnp.where(row < offset, edge[r], held[r, :half, :])

        @pl.when(offset < 0)
        def _(r=r, offset=offset):
            held[r, half:, :] = jnp.where(row >= half + offset, edge[r], held[r, half:, :])

        pltpu.make_async_copy(held.at[r], out_ref.at[r], write_sem.at[r]).start()
    for r in range(radii):
        pltpu.make_async_copy(held.at[r], out_ref.at[r], write_sem.at[r]).wait()


def patch(plan, steer, fields, from_last, from_next):
    radii = len(fields)
    cells, bins = fields[0].shape
    half = cells // 2
    anywhere = pl.BlockSpec(memory_space=pl.ANY)
    return pl.pallas_call(
        functools.partial(patch_kernel, plan, radii),
        grid_spec=pltpu.PrefetchScalarGridSpec(
            num_scalar_prefetch=1,
            grid=(),
            in_specs=[anywhere] * (radii + 2),
            out_specs=anywhere,
            scratch_shapes=[
                pltpu.VMEM((radii, cells, bins), jnp.float32),
                pltpu.VMEM((radii, half, bins), jnp.float32),
                pltpu.SemaphoreType.DMA((radii,)),
                pltpu.SemaphoreType.DMA((radii,)),
                pltpu.SemaphoreType.DMA((radii,)),
            ],
        ),
        out_shape=jax.ShapeDtypeStruct((radii, cells, bins), jnp.float32),
    )(steer, *fields, from_last, from_next)


def body(density, frag_rate, radial_speed, azimuth_speed, fraction, shifts, pivots):
    radii, cells, bins = density.shape
    count = lax.axis_size("phi")
    plan = Plan(radii)
    *fields, steer = step_cells(
        density, frag_rate, radial_speed, azimuth_speed, fraction, shifts, pivots, plan
    )
    hops = lax.rem(lax.div(shifts + cells // 2, cells), count)
    branches = [functools.partial(send, axis="phi", by=by) for by in range(count)]
    fields = [lax.switch(hops[r], branches, field) for r, field in enumerate(fields)]
    to_next, to_last = pack(plan, steer, fields)
    from_last = exchange(to_next, 1, 0, steer[plan.ahead_units])
    from_next = exchange(to_last, -1, cells // 2, steer[plan.behind_units])
    return patch(plan, steer, fields, from_last, from_next)


def solution(mesh):
    placed = (P("disc", "phi", None), P("disc", "phi"), P(), P(), P("disc"), P("disc"), P())
    return jax.shard_map(
        body, mesh=mesh, in_specs=placed, out_specs=P("disc", "phi", None), check_vma=False
    )
```
